32 devices in a mesh: front: 1, row: 16 (over z, y, x), col: 2 (over core).
Axes of the slice: x: 2, y: 2, z: 4, core: 2. Of those that a mesh axis runs over, the one named last changes fastest.
Arguments:
- contributions: float32 [16, 128, 4096], P(('front', 'row'), None, 'col'), may hold values from -0.176776695 to 0.176776695
- valid_rows: int32 [16], P(('front', 'row')), may hold values from 1 to 128, 1280 in all
Outputs:
- r_rows: float32 [512, 4096], P('front', 'col')
The draws below stay inside these ranges and needn't reach their ends.
All inputs are finite; a program needn't handle non-finite values. No bound on the sum of `valid_rows` on one device may be relied on, other than what follows from the above.
Results may differ from the reference program's by a relative error of at most 0.0003.
Values sent between devices are 32-bit elements; how exact they have to be, the bound alone decides.
A program may use at most 64 MiB of HBM per device.

```python
import math
import jax
import jax.numpy as jnp
import numpy as np
from jax import lax

W = 4096
PANEL = 256
NPANEL = 2
BLOCK = 128
NBLK = 16


def draw_contributions(key, part):
    full_shape = (NBLK, BLOCK, W)
    spread = 1.0 / math.sqrt(BLOCK * NBLK)
    base_key = jax.random.fold_in(jax.random.fold_in(key, 11), 0)
    block_pos = jnp.arange(NBLK, dtype=jnp.float32) / max(NBLK - 1, 1)
    base_draw = jnp.clip(jax.random.normal(base_key, full_shape, jnp.float32), -4.0, 4.0)
    block_scale = jnp.exp(math.log(3.0) * (block_pos - 1.0))
    leading = NPANEL * PANEL
    column_ids = jnp.arange(W, dtype=jnp.int32)
    shifted = jnp.concatenate([jnp.zeros((NBLK, BLOCK, 1), jnp.float32), base_draw[:, :, :-1]], axis=2)
    mixing = 0.5 * ((column_ids >= 1) & (column_ids < leading)).astype(jnp.float32)
    mixed_cols = (base_draw + mixing[None, None, :] * shifted) * block_scale[:, None, None] * spread
    return jnp.clip(mixed_cols, -8.0 * spread, 8.0 * spread)


def split_up(number_of, total, most, slope):
    portions = [(1 << 20) // math.isqrt(rank ** slope) + 1 for rank in range(2, number_of + 1)]
    surplus, counts = total - most - (number_of - 1), [1] * (number_of - 1)
    while surplus > 0:
        movable = [i for i in range(number_of - 1) if counts[i] < most]
        pool, remaining = sum([portions[i] for i in movable]), surplus
        for i in movable:
            more = min(most - counts[i], max(1, remaining * portions[i] // pool), surplus)
            counts[i] = counts[i] + more
            surplus = surplus - more
    return np.array([most] + counts)


def uneven(own_key, number_of, total, reach, slope):
    if number_of == 2:
        one = jax.random.randint(own_key, (), max(1, total - reach), min(reach, total - 1) + 1)
        return jnp.stack([one, total - one])
    tallies = jnp.asarray(split_up(number_of, total, reach, slope), jnp.int32)
    couples = (number_of - 1) // 2
    giver, sink = tallies[1:1 + 2 * couples:2], tallies[2:2 + 2 * couples:2]
    slack = jnp.minimum(giver - 1, reach - sink)
    moved = jax.random.randint(jax.random.fold_in(own_key, 1), (couples,), 0, 1 << 20) % (slack + 1)
    tallies = tallies.at[1:1 + 2 * couples:2].set(giver - moved).at[2:2 + 2 * couples:2].set(sink + moved)
    return tallies[jax.random.permutation(jax.random.fold_in(own_key, 2), number_of)]


def setup_inputs(seed: int = 0, part: int = 0) -> dict:
    key_of = jax.random.split(jax.random.key(seed), 3)
    part_keys = jax.random.split(jax.random.fold_in(key_of[2], part), 3)
    return {
        "contributions": draw_contributions(jax.random.fold_in(jax.random.fold_in(key_of[2], part), 71), part),
        "valid_rows": uneven(part_keys[1], NBLK, NBLK * 80, BLOCK, 2).astype(jnp.int32),
    }


def reference(contributions, valid_rows):
    blocks, height, width = contributions.shape
    live_rows = (jnp.arange(height, dtype=jnp.int32)[None, :] < valid_rows[:, None]).astype(jnp.float32)
    frontal = (contributions * live_rows[:, :, None]).reshape(blocks * height, width)
    leading = NPANEL * PANEL
    basis, triangle = jnp.linalg.qr(frontal[:, :leading])
    sign_fix = jnp.sign(jnp.diagonal(triangle))
    projected = jnp.dot(basis.T, frontal, precision=lax.Precision.HIGHEST) * sign_fix[:, None]
    kept_mask = jnp.arange(width, dtype=jnp.int32)[None, :] >= jnp.arange(leading, dtype=jnp.int32)[:, None]
    return jnp.where(kept_mask, projected, jnp.zeros_like(projected))
```

```python
import functools

import jax
import jax.numpy as jnp
from jax import lax
from jax.experimental import pallas as pl
from jax.experimental.pallas import tpu as pltpu
from jax.sharding import PartitionSpec as P

PANEL = 256
NPANEL = 2
LANES = 128
SUB = 8
HIGHEST = lax.Precision.HIGHEST
MESH = pl.DeviceIdType.MESH


def spread(block, axis, owner):
    block = jnp.where(lax.axis_index(axis) == owner, block, jnp.zeros_like(block))
    return lax.psum(block, axis)


def inner_cols(left, right):
    return jnp.einsum("rp,rc->pc", left, right, precision=HIGHEST)


def by_psum(frontal, leading):
    width_local = frontal.shape[1]
    leading_cols = spread(frontal[:, :leading], "col", 0)
    gram_total = lax.psum(inner_cols(leading_cols, leading_cols), "row")
    factor = jnp.linalg.cholesky(gram_total)
    identity = jnp.eye(leading, dtype=jnp.float32)
    inverse = jax.scipy.linalg.solve_triangular(factor, identity, lower=True)
    first_basis = jnp.dot(leading_cols, inverse.T, precision=HIGHEST)
    projected = lax.psum(inner_cols(first_basis, frontal), "row")
    column_ids = lax.axis_index("col") * width_local + jnp.arange(width_local, dtype=jnp.int32)
    kept_mask = column_ids[None, :] >= jnp.arange(leading, dtype=jnp.int32)[:, None]
    return jnp.where(kept_mask, projected, jnp.zeros_like(projected))


def dot_t(left, right):
    return lax.dot_general(
        left, right, (((0,), (0,)), ((), ())), precision=HIGHEST, preferred_element_type=jnp.float32
    )


def inverse_factor(read, hooks):
    groups = LANES // SUB
    row = lax.broadcasted_iota(jnp.int32, (SUB, LANES), 0)
    col = lax.broadcasted_iota(jnp.int32, (SUB, LANES), 1)
    a = [read(g) for g in range(groups)]
    b = [jnp.where(row + g * SUB == col, 1.0, 0.0).astype(jnp.float32) for g in range(groups)]
    scales = []
    for j in range(LANES):
        if j in hooks:
            hooks[j]()
        home, i = divmod(j, SUB)
        prow = a[home][i : i + 1, :]
        brow = b[home][i : i + 1, :]
        pinv = 1.0 / prow[:, j : j + 1]
        srow = prow * pinv
        trow = brow * pinv
        for g in range(home, groups):
            f = a[g][:, j : j + 1]
            if g == home:
                if i == SUB - 1:
                    continue
                f = jnp.where(row > i, jnp.broadcast_to(f, (SUB, LANES)), 0.0)
            a[g] = a[g] - f * srow
            b[g] = b[g] - f * trow
        if i == SUB - 1:
            diag = jnp.sum(jnp.where(row + home * SUB == col, a[home], 0.0), axis=1, keepdims=True)
            b[home] = b[home] * lax.rsqrt(diag)
    return b


def kernel(n, leading, f_ref, out_ref, a_all, f_all, gc, inv,
           own_sem, pair_send, pair_recv, ag_send, ag_recv, core_send, core_recv,
           x_send, x_recv, r_send, r_recv):
    height, width = f_ref.shape
    share = width // n
    half = height // 2
    chunks = leading // LANES
    stages = n.bit_length() - 1
    r = lax.axis_index("row")
    c = lax.axis_index("col")
    bits = [n >> (s + 1) for s in range(stages)]
    deltas = [b * (1 - 2 * (lax.rem(r // b, 2))) for b in bits]

    def ordered(parity):
        return deltas[:-2] + [
            deltas[-2] * (1 - parity) + deltas[-1] * parity,
            deltas[-1] * (1 - parity) + deltas[-2] * parity,
        ]

    def at(j, steps):
        place = r
        for s in range(stages):
            if (j >> s) & 1:
                place = place + steps[s]
        return place

    barrier = pltpu.get_barrier_semaphore()
    for d in range(1, n):
        pl.semaphore_signal(barrier, inc=1, device_id={"row": lax.rem(r + d, n)}, device_id_type=MESH)
    pl.semaphore_signal(barrier, inc=1, device_id={"col": 1 - c}, device_id_type=MESH)
    pl.semaphore_wait(barrier, n)

    mine = pl.ds(pl.multiple_of(r * height, height), height)
    lead = f_ref.at[:, pl.ds(0, leading)]
    own_lead = pltpu.make_async_copy(lead, a_all.at[mine, :], own_sem.at[0])
    to_pair = pltpu.make_async_remote_copy(
        src_ref=lead, dst_ref=a_all.at[mine, :], send_sem=pair_send, recv_sem=pair_recv,
        device_id={"col": 1 - c}, device_id_type=MESH,
    )

    @pl.when(c == 0)
    def _():
        to_pair.start()
        own_lead.start()
        own_lead.wait()

    @pl.when(c == 1)
    def _():
        to_pair.wait_recv()

    lead_steps = ordered(c)

    def lead_half(j, core):
        start = at(j, lead_steps) * height + core * half
        return a_all.at[pl.ds(pl.multiple_of(start, half), half), :]

    def lead_copy(j, s):
        return pltpu.make_async_remote_copy(
            src_ref=lead_half(j, c), dst_ref=lead_half(j, c),
            send_sem=ag_send.at[j + (1 << s)], recv_sem=ag_recv.at[j + (1 << s)],
            device_id={"row": r + lead_steps[s]}, device_id_type=MESH,
        )

    def core_copy(j):
        return pltpu.make_async_remote_copy(
            src_ref=lead_half(j, c), dst_ref=lead_half(j, c),
            send_sem=core_send.at[j], recv_sem=core_recv.at[j],
            device_id={"col": 1 - c}, device_id_type=MESH,
        )

    def share_copy(d):
        peer = lax.rem(r + d, n)
        return pltpu.make_async_remote_copy(
            src_ref=f_ref.at[:, pl.ds(pl.multiple_of(peer * share, share), share)],
            dst_ref=f_all.at[mine, :],
            send_sem=x_send.at[d], recv_sem=x_recv.at[d],
            device_id={"row": peer}, device_id_type=MESH,
        )

    for s in range(stages):
        lead_copy(0, s).start()
    own_share = pltpu.make_async_copy(
        f_ref.at[:, pl.ds(pl.multiple_of(r * share, share), share)], f_all.at[mine, :], own_sem.at[1]
    )
    own_share.start()
    for d in range(1, n):
        share_copy(d).start()
    for j in range(1, n):
        top = j.bit_length() - 1
        lead_copy(j - (1 << top), top).wait_recv()
        for s in range(top + 1, stages):
            lead_copy(j, s).start()
        core_copy(j).start()
    own_share.wait()
    for j in range(1, n):
        core_copy(j).wait_recv()
    for d in range(1, n):
        share_copy(d).wait_recv()

    step_rows = 4 * LANES
    gc[...] = jnp.zeros_like(gc)

    @pl.loop(0, (n * height) // step_rows)
    def _(t):
        rows = pl.ds(pl.multiple_of(t * step_rows, step_rows), step_rows)
        right = f_all[rows, :]
        for k in range(chunks):
            ks = pl.ds(k * LANES, LANES)
            left = a_all[rows, ks]
            rest = pl.ds(k * LANES, leading - k * LANES)
            gc[ks, rest] += dot_t(left, a_all[rows, rest])
            gc[ks, pl.ds(leading, share)] += dot_t(left, right)

    def out_piece(k, j, steps):
        cols = pl.ds(pl.multiple_of(at(j, steps) * share, share), share)
        return out_ref.at[pl.ds(pl.multiple_of(k * LANES, LANES), LANES), cols]

    def out_copy(k, j, s):
        steps = ordered(lax.rem(k, 2))
        return pltpu.make_async_remote_copy(
            src_ref=out_piece(k, j, steps), dst_ref=out_piece(k, j, steps),
            send_sem=r_send.at[k, j + (1 << s)], recv_sem=r_recv.at[k, j + (1 << s)],
            device_id={"row": r + steps[s]}, device_id_type=MESH,
        )

    def forward(k, top):
        for j in range(1 << top, 2 << top):
            out_copy(k, j - (1 << top), top).wait_recv()
            for s in range(top + 1, stages):
                out_copy(k, j, s).start()

    first_col = c * width + r * share
    row_id = lax.broadcasted_iota(jnp.int32, (LANES, share), 0)
    col_id = lax.broadcasted_iota(jnp.int32, (LANES, share), 1) + first_col

    @pl.loop(0, chunks)
    def _(k):
        base = pl.multiple_of(k * LANES, LANES)
        ks = pl.ds(base, LANES)

        def read(g):
            return gc[pl.ds(pl.multiple_of(base + g * SUB, SUB), SUB), ks]

        def hook(top):
            def run():
                @pl.when(k > 0)
                def _():
                    forward(k - 1, top)
            return run

        gap = LANES // stages
        hooks = {gap * (s + 1) - 1: hook(s) for s in range(stages)}
        b = inverse_factor(read, hooks)
        for g, part in enumerate(b):
            inv[pl.ds(g * SUB, SUB), :] = part
        rows = jnp.dot(inv[...], gc[ks, :], precision=HIGHEST, preferred_element_type=jnp.float32)
        mine_out = rows[:, leading:]
        out_ref[ks, pl.ds(pl.multiple_of(r * share, share), share)] = jnp.where(
            col_id >= row_id + base, mine_out, 0.0
        )
        for s in range(stages):
            out_copy(k, 0, s).start()
        gc[ks, :] = rows
        for i in range(1, chunks):
            @pl.when(i > k)
            def _():
                left = gc[ks, pl.ds(i * LANES, LANES)]
                rest = pl.ds(i * LANES, leading + share - i * LANES)
                gc[pl.ds(i * LANES, LANES), rest] -= dot_t(left, gc[ks, rest])

    for top in range(stages):
        forward(chunks - 1, top)

    @pl.when(c == 0)
    def _():
        to_pair.wait_send()

    for j in range(1, n):
        top = j.bit_length() - 1
        lead_copy(j - (1 << top), top).wait_send()
        core_copy(j).wait_send()
        share_copy(j).wait_send()
        for k in range(chunks):
            out_copy(k, j - (1 << top), top).wait_send()


def by_kernel(frontal, leading, n):
    height, width = frontal.shape
    share = width // n
    dma = pltpu.SemaphoreType.DMA
    return pl.pallas_call(
        functools.partial(kernel, n, leading),
        out_shape=jax.ShapeDtypeStruct((leading, width), jnp.float32),
        in_specs=[pl.BlockSpec(memory_space=pltpu.VMEM)],
        out_specs=pl.BlockSpec(memory_space=pltpu.VMEM),
        scratch_shapes=[
            pltpu.VMEM((n * height, leading), jnp.float32),
            pltpu.VMEM((n * height, share), jnp.float32),
            pltpu.VMEM((leading, leading + share), jnp.float32),
            pltpu.VMEM((LANES, LANES), jnp.float32),
            dma((2,)), dma, dma, dma((n,)), dma((n,)), dma((n,)), dma((n,)),
            dma((n,)), dma((n,)),
            dma((leading // LANES, n)), dma((leading // LANES, n)),
        ],
        compiler_params=pltpu.CompilerParams(
            collective_id=0, has_side_effects=True, vmem_limit_bytes=48 << 20
        ),
        name="front_rows",
    )(frontal)


def body(n, pair, contributions, valid_rows):
    blocks, height, width_local = contributions.shape
    live_rows = jnp.arange(height, dtype=jnp.int32)[None, :] < valid_rows[:, None]
    frontal = jnp.where(live_rows[:, :, None], contributions, 0.0).reshape(blocks * height, width_local)
    leading = NPANEL * PANEL
    rows = blocks * height
    fits = (
        pair == 2 and n >= 4 and n & (n - 1) == 0 and width_local % n == 0
        and width_local // n == LANES and rows == LANES and leading <= width_local
    )
    if fits:
        return by_kernel(frontal, leading, n)
    return by_psum(frontal, leading)


def solution(mesh):
    return jax.shard_map(
        functools.partial(body, mesh.shape["row"], mesh.shape["col"]),
        mesh=mesh,
        in_specs=(P(("front", "row"), None, "col"), P(("front", "row"))),
        out_specs=P("front", "col"),
        check_vma=False,
    )
```

```python
import functools

import jax
import jax.numpy as jnp
from jax import lax
from jax.experimental import pallas as pl
from jax.experimental.pallas import tpu as pltpu
from jax.sharding import PartitionSpec as P

PANEL = 256
NPANEL = 2
LANES = 128
SUB = 8
HIGHEST = lax.Precision.HIGHEST
MESH = pl.DeviceIdType.MESH


def spread(block, axis, owner):
    block = jnp.where(lax.axis_index(axis) == owner, block, jnp.zeros_like(block))
    return lax.psum(block, axis)


def inner_cols(left, right):
    return jnp.einsum("rp,rc->pc", left, right, precision=HIGHEST)


def by_psum(frontal, leading):
    width_local = frontal.shape[1]
    leading_cols = spread(frontal[:, :leading], "col", 0)
    gram_total = lax.psum(inner_cols(leading_cols, leading_cols), "row")
    factor = jnp.linalg.cholesky(gram_total)
    identity = jnp.eye(leading, dtype=jnp.float32)
    inverse = jax.scipy.linalg.solve_triangular(factor, identity, lower=True)
    first_basis = jnp.dot(leading_cols, inverse.T, precision=HIGHEST)
    projected = lax.psum(inner_cols(first_basis, frontal), "row")
    column_ids = lax.axis_index("col") * width_local + jnp.arange(width_local, dtype=jnp.int32)
    kept_mask = column_ids[None, :] >= jnp.arange(leading, dtype=jnp.int32)[:, None]
    return jnp.where(kept_mask, projected, jnp.zeros_like(projected))


def dot_t(left, right):
    return lax.dot_general(
        left, right, (((0,), (0,)), ((), ())), precision=HIGHEST, preferred_element_type=jnp.float32
    )


def inverse_factor(read, hooks):
    groups = LANES // SUB
    tile = (SUB, LANES)
    row = lax.broadcasted_iota(jnp.int32, tile, 0)
    col = lax.broadcasted_iota(jnp.int32, tile, 1)
    a = [read(g) for g in range(groups)]
    b = [jnp.where(row + g * SUB == col, 1.0, 0.0).astype(jnp.float32) for g in range(groups)]

    def columns(value, home):
        first = home * SUB
        return [jnp.broadcast_to(value[:, first + t : first + t + 1], tile) for t in range(SUB)]

    def across(value, t):
        return jnp.broadcast_to(value[t : t + 1, :], tile)

    for home in range(groups):
        if home in hooks:
            hooks[home]()
        f = columns(a[home], home)
        arow, brow = a[home], b[home]
        scaled, factors = [], []
        diag = f[0]
        for t in range(SUB):
            pinv = 1.0 / across(f[t], t)
            diag = jnp.where(row == t, f[t], diag)
            srow = across(arow, t) * pinv
            trow = across(brow, t) * pinv
            later = [across(f[u], t) * pinv for u in range(t + 1, SUB)]
            below = jnp.where(row > t, f[t], 0.0)
            for u in range(t + 1, SUB):
                f[u] = f[u] - below * later[u - t - 1]
            if t < SUB - 1:
                arow = arow - below * srow
                brow = brow - below * trow
            scaled.append((srow, trow))
            factors.append(later)
        b[home] = brow * lax.rsqrt(diag)
        for g in range(home + 1, groups):
            f = columns(a[g], home)
            for t in range(SUB):
                for u in range(t + 1, SUB):
                    f[u] = f[u] - f[t] * factors[t][u - t - 1]
                a[g] = a[g] - f[t] * scaled[t][0]
                b[g] = b[g] - f[t] * scaled[t][1]
    return b


def kernel(n, leading, f_ref, out_ref, a_all, f_all, gc, inv,
           own_sem, pair_send, pair_recv, ag_send, ag_recv, core_send, core_recv,
           x_send, x_recv, r_send, r_recv):
    height, width = f_ref.shape
    share = width // n
    half = height // 2
    chunks = leading // LANES
    stages = n.bit_length() - 1
    r = lax.axis_index("row")
    c = lax.axis_index("col")
    bits = [n >> (s + 1) for s in range(stages)]
    deltas = [b * (1 - 2 * (lax.rem(r // b, 2))) for b in bits]

    def ordered(parity):
        return deltas[:-2] + [
            deltas[-2] * (1 - parity) + deltas[-1] * parity,
            deltas[-1] * (1 - parity) + deltas[-2] * parity,
        ]

    def at(j, steps):
        place = r
        for s in range(stages):
            if (j >> s) & 1:
                place = place + steps[s]
        return place

    gc[...] = jnp.zeros_like(gc)
    barrier = pltpu.get_barrier_semaphore()
    for d in range(1, n):
        pl.semaphore_signal(barrier, inc=1, device_id={"row": lax.rem(r + d, n)}, device_id_type=MESH)
    pl.semaphore_signal(barrier, inc=1, device_id={"col": 1 - c}, device_id_type=MESH)
    pl.semaphore_wait(barrier, n)

    lead = f_ref.at[:, pl.ds(0, leading)]
    first = pl.ds(0, height)
    own_lead = pltpu.make_async_copy(lead, a_all.at[first, :], own_sem.at[0])
    to_pair = pltpu.make_async_remote_copy(
        src_ref=lead, dst_ref=a_all.at[first, :], send_sem=pair_send, recv_sem=pair_recv,
        device_id={"col": 1 - c}, device_id_type=MESH,
    )

    @pl.when(c == 0)
    def _():
        to_pair.start()
        own_lead.start()
        own_lead.wait()

    @pl.when(c == 1)
    def _():
        to_pair.wait_recv()

    lead_steps = ordered(c)
    quarter = 1 << (stages - 2)

    def lead_half(j):
        low = j & (quarter - 1)
        slot = low + ((j >> (stages - 2)) & 1) * quarter * (1 + c) + (j >> (stages - 1)) * quarter * (2 - c)
        return a_all.at[pl.ds(pl.multiple_of(slot * height + c * half, half), half), :]

    def lead_copy(j, s):
        k = j + (1 << s)
        return pltpu.make_async_remote_copy(
            src_ref=lead_half(j), dst_ref=lead_half(k), send_sem=ag_send.at[k], recv_sem=ag_recv.at[k],
            device_id={"row": r + lead_steps[s]}, device_id_type=MESH,
        )

    def core_copy(j):
        return pltpu.make_async_remote_copy(
            src_ref=lead_half(j), dst_ref=lead_half(j),
            send_sem=core_send.at[j], recv_sem=core_recv.at[j],
            device_id={"col": 1 - c}, device_id_type=MESH,
        )

    def share_copy(d):
        peer = at(d, deltas)
        return pltpu.make_async_remote_copy(
            src_ref=f_ref.at[:, pl.ds(pl.multiple_of(peer * share, share), share)],
            dst_ref=f_all.at[pl.ds(d * height, height), :],
            send_sem=x_send.at[d], recv_sem=x_recv.at[d],
            device_id={"row": peer}, device_id_type=MESH,
        )

    def take(j):
        top = j.bit_length() - 1
        lead_copy(j - (1 << top), top).wait_recv()
        for s in range(top + 1, stages):
            lead_copy(j, s).start()
        core_copy(j).start()

    def gram(q):
        rows = pl.ds(q * quarter * height, quarter * height)
        for k in range(chunks):
            ks = pl.ds(k * LANES, LANES)
            rest = pl.ds(k * LANES, leading - k * LANES)
            gc[ks, rest] += dot_t(a_all[rows, ks], a_all[rows, rest])

    for s in range(stages):
        lead_copy(0, s).start()
    own_share = pltpu.make_async_copy(
        f_ref.at[:, pl.ds(pl.multiple_of(r * share, share), share)], f_all.at[first, :], own_sem.at[1]
    )
    own_share.start()
    for j in range(1, 2 * quarter):
        take(j)
    for d in range(1, n):
        share_copy(d).start()
    for j in range(1, quarter):
        core_copy(j).wait_recv()
    gram(0)
    for j in range(2 * quarter, 3 * quarter):
        take(j)
    for j in range(quarter, 3 * quarter):
        core_copy(j).wait_recv()
    gram(1)
    for j in range(3 * quarter, n):
        take(j)
    gram(2)
    for j in range(3 * quarter, n):
        core_copy(j).wait_recv()
    gram(3)

    def products():
        own_share.wait()
        for d in range(1, n):
            share_copy(d).wait_recv()
        for q in range(n // quarter):
            rows = pl.ds(q * quarter * height, quarter * height)
            gc[:, pl.ds(leading, share)] += dot_t(a_all[rows, :], f_all[rows, :])

    def out_piece(k, j, steps):
        cols = pl.ds(pl.multiple_of(at(j, steps) * share, share), share)
        return out_ref.at[pl.ds(pl.multiple_of(k * LANES, LANES), LANES), cols]

    def out_copy(k, j, s):
        steps = ordered(lax.rem(k + c, 2))
        return pltpu.make_async_remote_copy(
            src_ref=out_piece(k, j, steps), dst_ref=out_piece(k, j, steps),
            send_sem=r_send.at[k, j + (1 << s)], recv_sem=r_recv.at[k, j + (1 << s)],
            device_id={"row": r + steps[s]}, device_id_type=MESH,
        )

    def forward(k, top):
        for j in range(1 << top, 2 << top):
            out_copy(k, j - (1 << top), top).wait_recv()
            for s in range(top + 1, stages):
                out_copy(k, j, s).start()

    first_col = c * width + r * share
    row_id = lax.broadcasted_iota(jnp.int32, (LANES, share), 0)
    col_id = lax.broadcasted_iota(jnp.int32, (LANES, share), 1) + first_col

    @pl.loop(0, chunks)
    def _(k):
        base = pl.multiple_of(k * LANES, LANES)
        ks = pl.ds(base, LANES)

        def read(g):
            return gc[pl.ds(pl.multiple_of(base + g * SUB, SUB), SUB), ks]

        def hook(top):
            def run():
                @pl.when(k > 0)
                def _():
                    forward(k - 1, top)
            return run

        groups = LANES // SUB
        hooks = {(groups * (s + 1)) // stages: hook(s) for s in range(stages - 1)}
        b = inverse_factor(read, hooks)
        for g, part in enumerate(b):
            inv[pl.ds(g * SUB, SUB), :] = part
        pl.when(k == 0)(products)
        rows = jnp.dot(inv[...], gc[ks, :], precision=HIGHEST, preferred_element_type=jnp.float32)
        mine_out = rows[:, leading:]
        out_ref[ks, pl.ds(pl.multiple_of(r * share, share), share)] = jnp.where(
            col_id >= row_id + base, mine_out, 0.0
        )
        for s in range(stages):
            out_copy(k, 0, s).start()
        gc[ks, :] = rows
        for i in range(1, chunks):
            @pl.when(i > k)
            def _():
                left = gc[ks, pl.ds(i * LANES, LANES)]
                rest = pl.ds(i * LANES, leading + share - i * LANES)
                gc[pl.ds(i * LANES, LANES), rest] -= dot_t(left, gc[ks, rest])

    for top in range(stages - 1):
        forward(chunks - 1, top)
    for k in range(chunks):
        forward(k, stages - 1)

    @pl.when(c == 0)
    def _():
        to_pair.wait_send()

    for j in range(1, n):
        top = j.bit_length() - 1
        lead_copy(j - (1 << top), top).wait_send()
        core_copy(j).wait_send()
        share_copy(j).wait_send()
        for k in range(chunks):
            out_copy(k, j - (1 << top), top).wait_send()


def by_kernel(frontal, leading, n):
    height, width = frontal.shape
    share = width // n
    dma = pltpu.SemaphoreType.DMA
    return pl.pallas_call(
        functools.partial(kernel, n, leading),
        out_shape=jax.ShapeDtypeStruct((leading, width), jnp.float32),
        in_specs=[pl.BlockSpec(memory_space=pltpu.VMEM)],
        out_specs=pl.BlockSpec(memory_space=pltpu.VMEM),
        scratch_shapes=[
            pltpu.VMEM((n * height, leading), jnp.float32),
            pltpu.VMEM((n * height, share), jnp.float32),
            pltpu.VMEM((leading, leading + share), jnp.float32),
            pltpu.VMEM((LANES, LANES), jnp.float32),
            dma((2,)), dma, dma, dma((n,)), dma((n,)), dma((n,)), dma((n,)),
            dma((n,)), dma((n,)),
            dma((leading // LANES, n)), dma((leading // LANES, n)),
        ],
        compiler_params=pltpu.CompilerParams(
            collective_id=0, has_side_effects=True, vmem_limit_bytes=48 << 20
        ),
        name="front_rows",
    )(frontal)


def body(n, pair, contributions, valid_rows):
    blocks, height, width_local = contributions.shape
    live_rows = jnp.arange(height, dtype=jnp.int32)[None, :] < valid_rows[:, None]
    frontal = jnp.where(live_rows[:, :, None], contributions, 0.0).reshape(blocks * height, width_local)
    leading = NPANEL * PANEL
    rows = blocks * height
    fits = (
        pair == 2 and n >= 4 and n & (n - 1) == 0 and width_local % n == 0
        and width_local // n == LANES and rows == LANES and leading <= width_local
    )
    if fits:
        return by_kernel(frontal, leading, n)
    return by_psum(frontal, leading)


def solution(mesh):
    return jax.shard_map(
        functools.partial(body, mesh.shape["row"], mesh.shape["col"]),
        mesh=mesh,
        in_specs=(P(("front", "row"), None, "col"), P(("front", "row"))),
        out_specs=P("front", "col"),
        check_vma=False,
    )
```

```python
import functools

import jax
import jax.numpy as jnp
from jax import lax
from jax.experimental import pallas as pl
from jax.experimental.pallas import tpu as pltpu
from jax.sharding import PartitionSpec as P

PANEL = 256
NPANEL = 2
LANES = 128
SUB = 8
HIGHEST = lax.Precision.HIGHEST
MESH = pl.DeviceIdType.MESH


def spread(block, axis, owner):
    block = jnp.where(lax.axis_index(axis) == owner, block, jnp.zeros_like(block))
    return lax.psum(block, axis)


def inner_cols(left, right):
    return jnp.einsum("rp,rc->pc", left, right, precision=HIGHEST)


def by_psum(frontal, leading):
    width_local = frontal.shape[1]
    leading_cols = spread(frontal[:, :leading], "col", 0)
    gram_total = lax.psum(inner_cols(leading_cols, leading_cols), "row")
    factor = jnp.linalg.cholesky(gram_total)
    identity = jnp.eye(leading, dtype=jnp.float32)
    inverse = jax.scipy.linalg.solve_triangular(factor, identity, lower=True)
    first_basis = jnp.dot(leading_cols, inverse.T, precision=HIGHEST)
    projected = lax.psum(inner_cols(first_basis, frontal), "row")
    column_ids = lax.axis_index("col") * width_local + jnp.arange(width_local, dtype=jnp.int32)
    kept_mask = column_ids[None, :] >= jnp.arange(leading, dtype=jnp.int32)[:, None]
    return jnp.where(kept_mask, projected, jnp.zeros_like(projected))


def dot_t(left, right):
    return lax.dot_general(
        left, right, (((0,), (0,)), ((), ())), precision=HIGHEST, preferred_element_type=jnp.float32
    )


def inverse_factor(read, hooks):
    groups = LANES // SUB
    tile = (SUB, LANES)
    row = lax.broadcasted_iota(jnp.int32, tile, 0)
    col = lax.broadcasted_iota(jnp.int32, tile, 1)
    a = [read(g) for g in range(groups)]
    b = [jnp.where(row + g * SUB == col, 1.0, 0.0).astype(jnp.float32) for g in range(groups)]

    def columns(value, home):
        first = home * SUB
        return [jnp.broadcast_to(value[:, first + t : first + t + 1], tile) for t in range(SUB)]

    def across(value, t):
        return jnp.broadcast_to(value[t : t + 1, :], tile)

    for home in range(groups):
        if home in hooks:
            hooks[home]()
        f = columns(a[home], home)
        arow, brow = a[home], b[home]
        scaled, factors = [], []
        diag = f[0]
        for t in range(SUB):
            pinv = 1.0 / across(f[t], t)
            diag = jnp.where(row == t, f[t], diag)
            srow = across(arow, t) * pinv
            trow = across(brow, t) * pinv
            later = [across(f[u], t) * pinv for u in range(t + 1, SUB)]
            below = jnp.where(row > t, f[t], 0.0)
            for u in range(t + 1, SUB):
                f[u] = f[u] - below * later[u - t - 1]
            if t < SUB - 1:
                arow = arow - below * srow
                brow = brow - below * trow
            scaled.append((srow, trow))
            factors.append(later)
        b[home] = brow * lax.rsqrt(diag)
        for g in range(home + 1, groups):
            f = columns(a[g], home)
            for t in range(SUB):
                for u in range(t + 1, SUB):
                    f[u] = f[u] - f[t] * factors[t][u - t - 1]
                a[g] = a[g] - f[t] * scaled[t][0]
                b[g] = b[g] - f[t] * scaled[t][1]
    return b


def kernel(n, leading, f_ref, out_ref, a_all, f_all, gc, inv,
           own_sem, pair_send, pair_recv, ag_send, ag_recv, core_send, core_recv,
           x_send, x_recv, r_send, r_recv):
    height, width = f_ref.shape
    share = width // n
    half = height // 2
    chunks = leading // LANES
    stages = n.bit_length() - 1
    r = lax.axis_index("row")
    c = lax.axis_index("col")
    bits = [n >> (s + 1) for s in range(stages)]
    deltas = [b * (1 - 2 * (lax.rem(r // b, 2))) for b in bits]

    def ordered(parity):
        return deltas[:-2] + [
            deltas[-2] * (1 - parity) + deltas[-1] * parity,
            deltas[-1] * (1 - parity) + deltas[-2] * parity,
        ]

    def at(j, steps):
        place = r
        for s in range(stages):
            if (j >> s) & 1:
                place = place + steps[s]
        return place

    gc[...] = jnp.zeros_like(gc)
    barrier = pltpu.get_barrier_semaphore()
    for d in range(1, n):
        pl.semaphore_signal(barrier, inc=1, device_id={"row": lax.rem(r + d, n)}, device_id_type=MESH)
    pl.semaphore_signal(barrier, inc=1, device_id={"col": 1 - c}, device_id_type=MESH)
    pl.semaphore_wait(barrier, n)

    lead = f_ref.at[:, pl.ds(0, leading)]
    first = pl.ds(0, height)
    own_lead = pltpu.make_async_copy(lead, a_all.at[first, :], own_sem.at[0])
    to_pair = pltpu.make_async_remote_copy(
        src_ref=lead, dst_ref=a_all.at[first, :], send_sem=pair_send, recv_sem=pair_recv,
        device_id={"col": 1 - c}, device_id_type=MESH,
    )

    @pl.when(c == 0)
    def _():
        to_pair.start()
        own_lead.start()
        own_lead.wait()

    @pl.when(c == 1)
    def _():
        to_pair.wait_recv()

    lead_steps = ordered(c)
    quarter = 1 << (stages - 2)

    def lead_half(j):
        low = j & (quarter - 1)
        slot = low + ((j >> (stages - 2)) & 1) * quarter * (1 + c) + (j >> (stages - 1)) * quarter * (2 - c)
        return a_all.at[pl.ds(pl.multiple_of(slot * height + c * half, half), half), :]

    def lead_copy(j, s):
        k = j + (1 << s)
        return pltpu.make_async_remote_copy(
            src_ref=lead_half(j), dst_ref=lead_half(k), send_sem=ag_send.at[k], recv_sem=ag_recv.at[k],
            device_id={"row": r + lead_steps[s]}, device_id_type=MESH,
        )

    def core_copy(j):
        return pltpu.make_async_remote_copy(
            src_ref=lead_half(j), dst_ref=lead_half(j),
            send_sem=core_send.at[j], recv_sem=core_recv.at[j],
            device_id={"col": 1 - c}, device_id_type=MESH,
        )

    def share_copy(d):
        peer = at(d, deltas)
        return pltpu.make_async_remote_copy(
            src_ref=f_ref.at[:, pl.ds(pl.multiple_of(peer * share, share), share)],
            dst_ref=f_all.at[pl.ds(d * height, height), :],
            send_sem=x_send.at[d], recv_sem=x_recv.at[d],
            device_id={"row": peer}, device_id_type=MESH,
        )

    def take(j):
        top = j.bit_length() - 1
        lead_copy(j - (1 << top), top).wait_recv()
        for s in range(top + 1, stages):
            lead_copy(j, s).start()
        core_copy(j).start()

    def gram(q):
        rows = pl.ds(q * quarter * height, quarter * height)
        for k in range(chunks):
            ks = pl.ds(k * LANES, LANES)
            rest = pl.ds(k * LANES, leading - k * LANES)
            gc[ks, rest] += dot_t(a_all[rows, ks], a_all[rows, rest])

    for s in range(stages):
        lead_copy(0, s).start()
    own_share = pltpu.make_async_copy(
        f_ref.at[:, pl.ds(pl.multiple_of(r * share, share), share)], f_all.at[first, :], own_sem.at[1]
    )
    own_share.start()
    for j in range(1, 2 * quarter):
        take(j)
    for d in range(1, n):
        share_copy(d).start()
    for j in range(1, quarter):
        core_copy(j).wait_recv()
    gram(0)
    for j in range(2 * quarter, 3 * quarter):
        take(j)
    for j in range(quarter, 3 * quarter):
        core_copy(j).wait_recv()
    gram(1)
    for j in range(3 * quarter, n):
        take(j)
    gram(2)
    for j in range(3 * quarter, n):
        core_copy(j).wait_recv()
    gram(3)

    def products():
        own_share.wait()
        for d in range(1, n):
            share_copy(d).wait_recv()
        for q in range(n // quarter):
            rows = pl.ds(q * quarter * height, quarter * height)
            gc[:, pl.ds(leading, share)] += dot_t(a_all[rows, :], f_all[rows, :])

    def out_piece(k, j, steps):
        cols = pl.ds(pl.multiple_of(at(j, steps) * share, share), share)
        return out_ref.at[pl.ds(pl.multiple_of(k * LANES, LANES), LANES), cols]

    def out_copy(k, j, s):
        steps = ordered(lax.rem(k + c, 2))
        return pltpu.make_async_remote_copy(
            src_ref=out_piece(k, j, steps), dst_ref=out_piece(k, j, steps),
            send_sem=r_send.at[k, j + (1 << s)], recv_sem=r_recv.at[k, j + (1 << s)],
            device_id={"row": r + steps[s]}, device_id_type=MESH,
        )

    def forward(k, top):
        for j in range(1 << top, 2 << top):
            out_copy(k, j - (1 << top), top).wait_recv()
            for s in range(top + 1, stages):
                out_copy(k, j, s).start()

    first_col = c * width + r * share
    row_id = lax.broadcasted_iota(jnp.int32, (LANES, share), 0)
    col_id = lax.broadcasted_iota(jnp.int32, (LANES, share), 1) + first_col

    @pl.loop(0, chunks)
    def _(k):
        base = pl.multiple_of(k * LANES, LANES)
        ks = pl.ds(base, LANES)

        def read(g):
            return gc[pl.ds(pl.multiple_of(base + g * SUB, SUB), SUB), ks]

        def hook(back, top):
            def run():
                @pl.when(k >= back)
                def _():
                    forward(k - back, top)
            return run

        groups = LANES // SUB
        hooks = {2: hook(2, stages - 2)}
        for s in range(stages - 2):
            hooks[groups * (s + 1) // (stages - 1) + 1] = hook(1, s)
        b = inverse_factor(read, hooks)
        for g, part in enumerate(b):
            inv[pl.ds(g * SUB, SUB), :] = part
        pl.when(k == 0)(products)
        rows = jnp.dot(inv[...], gc[ks, :], precision=HIGHEST, preferred_element_type=jnp.float32)
        mine_out = rows[:, leading:]
        out_ref[ks, pl.ds(pl.multiple_of(r * share, share), share)] = jnp.where(
            col_id >= row_id + base, mine_out, 0.0
        )
        for s in range(stages):
            out_copy(k, 0, s).start()
        gc[ks, :] = rows
        for i in range(1, chunks):
            @pl.when(i > k)
            def _():
                left = gc[ks, pl.ds(i * LANES, LANES)]
                rest = pl.ds(i * LANES, leading + share - i * LANES)
                gc[pl.ds(i * LANES, LANES), rest] -= dot_t(left, gc[ks, rest])

    forward(chunks - 2, stages - 2)
    for top in range(stages - 1):
        forward(chunks - 1, top)
    for k in range(chunks):
        forward(k, stages - 1)

    @pl.when(c == 0)
    def _():
        to_pair.wait_send()

    for j in range(1, n):
        top = j.bit_length() - 1
        lead_copy(j - (1 << top), top).wait_send()
        core_copy(j).wait_send()
        share_copy(j).wait_send()
        for k in range(chunks):
            out_copy(k, j - (1 << top), top).wait_send()


def by_kernel(frontal, leading, n):
    height, width = frontal.shape
    share = width // n
    dma = pltpu.SemaphoreType.DMA
    return pl.pallas_call(
        functools.partial(kernel, n, leading),
        out_shape=jax.ShapeDtypeStruct((leading, width), jnp.float32),
        in_specs=[pl.BlockSpec(memory_space=pltpu.VMEM)],
        out_specs=pl.BlockSpec(memory_space=pltpu.VMEM),
        scratch_shapes=[
            pltpu.VMEM((n * height, leading), jnp.float32),
            pltpu.VMEM((n * height, share), jnp.float32),
            pltpu.VMEM((leading, leading + share), jnp.float32),
            pltpu.VMEM((LANES, LANES), jnp.float32),
            dma((2,)), dma, dma, dma((n,)), dma((n,)), dma((n,)), dma((n,)),
            dma((n,)), dma((n,)),
            dma((leading // LANES, n)), dma((leading // LANES, n)),
        ],
        compiler_params=pltpu.CompilerParams(
            collective_id=0, has_side_effects=True, vmem_limit_bytes=48 << 20
        ),
        name="front_rows",
    )(frontal)


def body(n, pair, contributions, valid_rows):
    blocks, height, width_local = contributions.shape
    live_rows = jnp.arange(height, dtype=jnp.int32)[None, :] < valid_rows[:, None]
    frontal = jnp.where(live_rows[:, :, None], contributions, 0.0).reshape(blocks * height, width_local)
    leading = NPANEL * PANEL
    rows = blocks * height
    fits = (
        pair == 2 and n >= 4 and n & (n - 1) == 0 and width_local % n == 0
        and width_local // n == LANES and rows == LANES and leading <= width_local
    )
    if fits:
        return by_kernel(frontal, leading, n)
    return by_psum(frontal, leading)


def solution(mesh):
    return jax.shard_map(
        functools.partial(body, mesh.shape["row"], mesh.shape["col"]),
        mesh=mesh,
        in_specs=(P(("front", "row"), None, "col"), P(("front", "row"))),
        out_specs=P("front", "col"),
        check_vma=False,
    )
```
